512 devices in a mesh: dp: 2 (over x_lo), row: 16 (over x_hi, y), col: 16 (over z, core).
Axes of the slice: x: 4 (x_hi: 2, x_lo: 2; x = x_hi * 2 + x_lo), y: 8, z: 8, core: 2. Of those that a mesh axis runs over, the one named last changes fastest.
Arguments:
- tokens: bfloat16 [320, 8192], P('dp', 'row'), may hold values from -6 to 6
- cotangent: bfloat16 [320, 8192], P('dp', 'row'), may hold values from -6 to 6
- up_weight: bfloat16 [8192, 28672], P('row', ('dp', 'col')), may hold values from -0.0625 to 0.0625
- down_weight: bfloat16 [28672, 8192], P(('dp', 'col'), 'row'), may hold values from -0.03125 to 0.03125
Outputs:
- output: bfloat16 [320, 8192], P(('dp', 'col'), 'row')
- input_grad: bfloat16 [320, 8192], P(('dp', 'col'), 'row')
- up_grad: bfloat16 [8192, 28672], P('row', ('dp', 'col'))
- down_grad: bfloat16 [28672, 8192], P(('dp', 'col'), 'row')
The draws below stay inside these ranges and needn't reach their ends.
All inputs are finite; a program needn't handle non-finite values.
Results may differ from the reference program's by a relative error of at most 0.0061.
Values may be sent and summed in bfloat16 or wider, within the bound.
No kernel may reach another device: no remote copies, remote signals or barrier semaphores. Data moves between devices by JAX's collectives and lax.ppermute only.
A program may use at most 64 MiB of HBM per device.

```python
import jax
import jax.numpy as jnp
from jax import lax

D = 8192
FF = 28672
TOKENS = 320


def block_levels(key, extent, pieces, low, top_value):
    gain, own = 1.0, jax.random.fold_in(key, 6)
    for axis_at, shards_of in pieces:
        draws = jnp.exp(jax.random.uniform(jax.random.fold_in(own, axis_at), (shards_of,), jnp.float32, low / len(pieces), top_value / len(pieces)))
        gain = gain * jnp.repeat(draws, extent[axis_at] // shards_of).reshape([-1 if axis == axis_at else 1 for axis in range(len(extent))])
    return gain


def noise(own_key, dims, width, reach, cuts=(), kind=jnp.bfloat16):
    entries = jax.random.normal(own_key, dims, jnp.float32) * width
    if len(cuts) > 0:
        entries = block_levels(own_key, dims, cuts, -0.22, 0.18) * entries
    return jnp.clip(entries, min=-reach, max=reach).astype(kind)


def setup_inputs(seed: int = 0) -> dict:
    key_of = jax.random.split(jax.random.key(seed), 5)
    return {
        "tokens": noise(key_of[0], (TOKENS, D), 1.0, 6.0, ((0, 2), (1, 16))),
        "cotangent": noise(key_of[1], (TOKENS, D), 1.0, 6.0, ((0, 2), (1, 16))),
        "up_weight": noise(key_of[2], (D, FF), D ** -0.5, 0.0625, ((0, 16), (1, 32))),
        "down_weight": noise(key_of[3], (FF, D), FF ** -0.5, 0.03125, ((0, 32), (1, 16))),
    }


def reference(tokens, cotangent, up_weight, down_weight):
    preact = jnp.dot(tokens, up_weight, preferred_element_type=jnp.float32).astype(jnp.bfloat16)
    pre_wide = lax.optimization_barrier(preact).astype(jnp.float32)
    hidden = jax.nn.silu(pre_wide).astype(jnp.bfloat16)
    output = jnp.dot(hidden, down_weight, preferred_element_type=jnp.float32).astype(jnp.bfloat16)
    grad_hidden = lax.dot_general(cotangent, down_weight, (((1,), (1,)), ((), ())), preferred_element_type=jnp.float32).astype(jnp.bfloat16)
    sigma = jax.nn.sigmoid(pre_wide)
    slope = sigma * (1.0 + pre_wide * (1.0 - sigma))
    grad_pre = (lax.optimization_barrier(grad_hidden).astype(jnp.float32) * slope).astype(jnp.bfloat16)
    input_grad = lax.dot_general(grad_pre, up_weight, (((1,), (1,)), ((), ())), preferred_element_type=jnp.float32).astype(jnp.bfloat16)
    up_grad = lax.dot_general(tokens, grad_pre, (((0,), (0,)), ((), ())), preferred_element_type=jnp.float32).astype(jnp.bfloat16)
    down_grad = lax.dot_general(hidden, cotangent, (((0,), (0,)), ((), ())), preferred_element_type=jnp.float32).astype(jnp.bfloat16)
    return (output, input_grad, up_grad, down_grad)
```

```python
import jax
import jax.numpy as jnp
from jax import lax
from jax.sharding import Mesh, PartitionSpec as P

ROW = ("xh", "y")
f32, bf16 = jnp.float32, jnp.bfloat16


def silu_slope(pre_wide):
    sigma = jax.nn.sigmoid(pre_wide)
    return sigma * (1.0 + pre_wide * (1.0 - sigma))


def dot(a, b, dims):
    return lax.dot_general(a, b, (dims, ((), ())), preferred_element_type=f32)


def body(tokens, cotangent, up_weight, down_weight):
    both = lax.all_gather(jnp.stack([tokens, cotangent]), "dp", axis=1, tiled=True)
    acts, cots = both[0], both[1]
    count, hid = acts.shape[0], up_weight.shape[1]
    width = acts.shape[1]
    rows = count // 16
    up_part = dot(acts, up_weight, ((1,), (0,))).astype(bf16)
    back_part = dot(cots, down_weight, ((1,), (1,))).astype(bf16)
    parts = jnp.concatenate([up_part.reshape(16, rows, hid), back_part.reshape(16, rows, hid)], axis=1)
    parts = lax.all_to_all(parts, ROW, 0, 0, tiled=True)
    sums = jnp.sum(parts.astype(f32), axis=0).astype(bf16)
    pre_wide = sums[:rows].astype(f32)
    hidden = jax.nn.silu(pre_wide).astype(bf16)
    grad_pre = (sums[rows:].astype(f32) * silu_slope(pre_wide)).astype(bf16)
    mine = jnp.concatenate([hidden, grad_pre], axis=0)
    full = lax.all_to_all(jnp.broadcast_to(mine, (16,) + mine.shape), ROW, 0, 0, tiled=True)
    hidden = full[:, :rows].reshape(count, hid)
    grad_pre = full[:, rows:].reshape(count, hid)
    out_part = dot(hidden, down_weight, ((1,), (0,))).astype(bf16)
    in_part = dot(grad_pre, up_weight, ((1,), (1,))).astype(bf16)
    mini = count // 32
    parts = jnp.stack([out_part.reshape(16, 2, mini, width), in_part.reshape(16, 2, mini, width)], axis=2)
    parts = jnp.moveaxis(parts, 1, 0)
    parts = lax.all_to_all(parts, "c", 0, 0, tiled=True)
    parts = jnp.sum(parts.astype(f32), axis=0).astype(bf16)
    parts = lax.all_to_all(parts, ("dp", "z"), 0, 0, tiled=True)
    sums = jnp.sum(parts.astype(f32), axis=0).astype(bf16)
    up_grad = dot(acts, grad_pre, ((0,), (0,))).astype(bf16)
    down_grad = dot(hidden, cots, ((0,), (0,))).astype(bf16)
    return sums[0], sums[1], up_grad, down_grad


def solution(mesh):
    fine = Mesh(mesh.devices.reshape(2, 2, 8, 8, 2), ("dp", "xh", "y", "z", "c"))
    split = ("dp", "z", "c")
    acts, up, down = P("dp", ROW), P(ROW, split), P(split, ROW)
    return jax.shard_map(
        body,
        mesh=fine,
        in_specs=(acts, acts, up, down),
        out_specs=(down, down, up, down),
        check_vma=False,
    )
```

```python
import jax
import jax.numpy as jnp
from jax import lax
from jax.sharding import Mesh, PartitionSpec as P

ROW = ("xh", "y")
f32, bf16 = jnp.float32, jnp.bfloat16


def silu_slope(pre_wide):
    sigma = jax.nn.sigmoid(pre_wide)
    return sigma * (1.0 + pre_wide * (1.0 - sigma))


def dot(a, b, dims):
    return lax.dot_general(a, b, (dims, ((), ())), preferred_element_type=f32)


def add_up(parts):
    terms = [parts[i].astype(f32) for i in range(parts.shape[0])]
    while len(terms) > 1:
        terms = [a + b for a, b in zip(terms[::2], terms[1::2])]
    return terms[0]


def pick(first, low, high):
    return jnp.where(first, low, high), jnp.where(first, high, low)


def partials(acts, cots, up_weight, down_weight):
    rows = acts.shape[0] // 16
    up_part = dot(acts, up_weight, ((1,), (0,))).astype(bf16)
    back_part = dot(cots, down_weight, ((1,), (1,))).astype(bf16)
    return jnp.concatenate([up_part.reshape(16, rows, -1), back_part.reshape(16, rows, -1)], axis=1)


def activate(sums):
    rows = sums.shape[0] // 2
    sums = sums.astype(bf16).astype(f32)
    pre_wide = sums[:rows]
    hidden = jax.nn.silu(pre_wide).astype(bf16)
    grad_pre = (sums[rows:] * silu_slope(pre_wide)).astype(bf16)
    return jnp.concatenate([hidden, grad_pre], axis=0)


def unpack(full):
    rows = full.shape[1] // 2
    return full[:, :rows].reshape(-1, full.shape[2]), full[:, rows:].reshape(-1, full.shape[2])


def trade(parts, axis):
    return lax.all_to_all(parts, axis, 0, 0, tiled=True)


def copies(mine, count):
    return jnp.broadcast_to(mine, (count,) + mine.shape)


def body(tokens, cotangent, up_weight, down_weight):
    swap = [(0, 1), (1, 0)]
    at_dp, at_x, at_c = (lax.axis_index(n) == 0 for n in ("dp", "xh", "c"))
    far_acts = lax.ppermute(tokens, "dp", swap)
    far_cots = lax.ppermute(cotangent, "dp", swap)
    near = trade(partials(tokens, cotangent, up_weight, down_weight), ROW)
    far = partials(far_acts, far_cots, up_weight, down_weight)
    keep, send = pick(at_x, far[:8], far[8:])
    far = (keep.astype(f32) + lax.ppermute(send, "xh", swap).astype(f32)).astype(bf16)
    near, far = lax.optimization_barrier((near, far))
    far = trade(far, "y")
    near = activate(add_up(near))
    far = trade(copies(activate(add_up(far)), 8), "y")
    near, far = lax.optimization_barrier((near, far))
    other = lax.ppermute(far, "xh", swap)
    near = trade(copies(near, 16), ROW)
    far = jnp.concatenate(pick(at_x, far, other), axis=0)
    acts, cots = jnp.concatenate([tokens, far_acts]), jnp.concatenate([cotangent, far_cots])
    hidden, grad_pre = (jnp.concatenate(p) for p in zip(unpack(near), unpack(far)))
    out_part = dot(hidden, down_weight, ((1,), (0,))).astype(bf16)
    in_part = dot(grad_pre, up_weight, ((1,), (1,))).astype(bf16)
    ends = jnp.concatenate([out_part, in_part], axis=1)
    count, width = tokens.shape
    ends = jnp.concatenate(pick(at_dp, ends[:count], ends[count:]))
    ends = ends.reshape(16, 2, count // 16, 2 * width)
    keep, send = pick(at_c, ends[:, 0], ends[:, 1])
    ends = (keep.astype(f32) + lax.ppermute(send, "c", swap).astype(f32)).astype(bf16)
    sums = add_up(trade(ends, ("dp", "z"))).astype(bf16)
    up_grad = dot(acts, grad_pre, ((0,), (0,))).astype(bf16)
    down_grad = dot(hidden, cots, ((0,), (0,))).astype(bf16)
    return sums[:, :width], sums[:, width:], up_grad, down_grad


def solution(mesh):
    fine = Mesh(mesh.devices.reshape(2, 2, 8, 8, 2), ("dp", "xh", "y", "z", "c"))
    split = ("dp", "z", "c")
    acts, up, down = P("dp", ROW), P(ROW, split), P(split, ROW)
    return jax.shard_map(
        body,
        mesh=fine,
        in_specs=(acts, acts, up, down),
        out_specs=(down, down, up, down),
        check_vma=False,
    )
```

```python
import jax
import jax.numpy as jnp
from jax import lax
from jax.experimental import pallas as pl
from jax.experimental.pallas import tpu as pltpu
from jax.sharding import Mesh, PartitionSpec as P

ROW = ("xh", "y")
SWAP = [(0, 1), (1, 0)]
f32, bf16 = jnp.float32, jnp.bfloat16
SDS = jax.ShapeDtypeStruct


def dot(a, b, dims):
    return lax.dot_general(a, b, (dims, ((), ())), preferred_element_type=f32)


def call(kernel, outs, *args):
    spaces = [pltpu.SMEM if a.dtype == jnp.int32 else pltpu.VMEM for a in args]
    return pl.pallas_call(
        kernel,
        out_shape=outs,
        in_specs=[pl.BlockSpec(memory_space=s) for s in spaces],
        compiler_params=pltpu.CompilerParams(vmem_limit_bytes=24 * 2**20),
    )(*args)


def low(shape):
    return lax.broadcasted_iota(jnp.int32, shape, 0) < 4


def order_kernel(tokens_ref, cots_ref, out_ref):
    n = tokens_ref.shape[0]
    i = lax.broadcasted_iota(jnp.int32, (n, n), 0)
    t = lax.broadcasted_iota(jnp.int32, (n, n), 1)
    k = i - n * 4 // 5
    source = jnp.where(k < 0, 10 * (i >> 3) + (i & 7), 10 * (k >> 1) + 8 + (k & 1))
    pick = (source == t).astype(f32).astype(bf16)
    out_ref[:n] = dot(pick, tokens_ref[...], ((1,), (0,))).astype(bf16)
    out_ref[n:] = dot(pick, cots_ref[...], ((1,), (0,))).astype(bf16)


def partial_kernel(both_ref, up_ref, down_ref, out_ref):
    for d in range(2):
        base = 320 * d
        up = dot(both_ref[base : base + 160], up_ref[...], ((1,), (0,)))
        back = dot(both_ref[base + 160 : base + 320], down_ref[...], ((1,), (1,)))
        for k in range(8):
            out_ref[8 * d + k, 0:16] = up[16 * k : 16 * k + 16].astype(bf16)
            out_ref[8 * d + k, 16:32] = back[16 * k : 16 * k + 16].astype(bf16)
        for k in range(0, 8, 2):
            u, b = up[128 + 4 * k : 136 + 4 * k], back[128 + 4 * k : 136 + 4 * k]
            first = low(u.shape)
            out_ref[8 * d + k, 32:40] = jnp.where(first, u, pltpu.roll(b, 4, 0)).astype(bf16)
            out_ref[8 * d + k + 1, 32:40] = jnp.where(first, pltpu.roll(u, 4, 0), b).astype(bf16)


def gate(pre, back):
    sigma = 1.0 / (1.0 + jnp.exp(-pre))
    return pre * sigma, back * (sigma * (1.0 + pre * (1.0 - sigma)))


def activate_kernel(parts_ref, out_ref):
    terms = [parts_ref[i].astype(f32) for i in range(16)]
    while len(terms) > 1:
        terms = [a + b for a, b in zip(terms[::2], terms[1::2])]
    sums = terms[0].astype(bf16).astype(f32)
    hidden, grad = gate(sums[0:16], sums[16:32])
    tail = sums[32:40]
    tail_hidden, tail_grad = gate(tail, pltpu.roll(tail, 4, 0))
    tail = jnp.where(low(tail.shape), tail_hidden, pltpu.roll(tail_grad, 4, 0)).astype(bf16)
    hidden, grad = hidden.astype(bf16), grad.astype(bf16)
    for i in range(16):
        out_ref[i, 0:16] = hidden
        out_ref[i, 16:32] = grad
        out_ref[i, 32:40] = tail


def ends_kernel(core_ref, full_ref, up_ref, down_ref, hid_ref, grad_ref, keep_ref, send_ref):
    for d in range(2):
        base = 160 * d
        for k in range(8):
            hid_ref[base + 16 * k : base + 16 * k + 16] = full_ref[8 * d + k, 0:16]
            grad_ref[base + 16 * k : base + 16 * k + 16] = full_ref[8 * d + k, 16:32]
        for k in range(0, 8, 4):
            hids, grads = [], []
            for j in (0, 2):
                even = full_ref[8 * d + k + j, 32:40].astype(f32)
                odd = full_ref[8 * d + k + j + 1, 32:40].astype(f32)
                first = low(even.shape)
                hids.append(jnp.where(first, even, pltpu.roll(odd, 4, 0)))
                grads.append(jnp.where(first, pltpu.roll(even, 4, 0), odd))
            at = base + 128 + 4 * k
            hid_ref[at : at + 16] = jnp.concatenate(hids).astype(bf16)
            grad_ref[at : at + 16] = jnp.concatenate(grads).astype(bf16)
    near = core_ref[0] == 0
    pair = lax.broadcasted_iota(jnp.int32, (8, 128), 0) >> 1
    for d in range(2):
        rows = slice(160 * d, 160 * d + 160)
        out = dot(hid_ref[rows], down_ref[...], ((1,), (0,)))
        inp = dot(grad_ref[rows], up_ref[...], ((1,), (1,)))
        for k in range(8):
            r = 8 * d + k
            at = 128 + 8 * (k // 2)
            for part, full in enumerate((out, inp)):
                tails = [jnp.zeros((8, 128), f32)] * 2
                for l in range(4):
                    lanes = slice(128 * l, 128 * l + 128)
                    to = 32 * part + 8 * l
                    a, b = full[16 * k : 16 * k + 8, lanes], full[16 * k + 8 : 16 * k + 16, lanes]
                    keep_ref[r, to : to + 8] = jnp.where(near, a, b)
                    send_ref[r, to : to + 8] = jnp.where(near, b, a).astype(bf16)
                    tile = full[at : at + 8, lanes]
                    for c in range(2):
                        shift = (2 * l - 2 * c - 4 * (k % 2)) % 8
                        moved = pltpu.roll(tile, shift, 0) if shift else tile
                        tails[c] = jnp.where(pair == l, moved, tails[c])
                to = 64 + 8 * part
                keep_ref[r, to : to + 8] = jnp.where(near, tails[0], tails[1])
                send_ref[r, to : to + 8] = jnp.where(near, tails[1], tails[0]).astype(bf16)


def total_kernel(parts_ref, out_ref, inp_ref):
    terms = [parts_ref[i].astype(f32) for i in range(16)]
    while len(terms) > 1:
        terms = [a + b for a, b in zip(terms[::2], terms[1::2])]
    sums = terms[0]
    for part, ref in enumerate((out_ref, inp_ref)):
        tail = sums[64 + 8 * part : 72 + 8 * part]
        for l in range(4):
            to = 32 * part + 8 * l
            last = pltpu.roll(tail, 8 - 2 * l, 0) if l else tail
            rows = jnp.concatenate([sums[to : to + 8], last]).astype(bf16)
            ref[:, 128 * l : 128 * l + 128] = rows[:10]


def trade(parts, axis):
    return lax.all_to_all(parts, axis, 0, 0, tiled=True)


def body(tokens, cotangent, up_weight, down_weight):
    core = lax.axis_index("c")[None]
    count, width = tokens.shape
    hid = up_weight.shape[1]
    both = call(order_kernel, SDS((2 * count, width), bf16), tokens, cotangent)
    both, core = lax.optimization_barrier((lax.all_gather(both, "dp", axis=0, tiled=True), core))
    slabs = SDS((16, 40, hid), bf16)
    parts = trade(call(partial_kernel, slabs, both, up_weight, down_weight), ROW)
    full = trade(call(activate_kernel, slabs, parts), ROW)
    rows = SDS((2 * count, hid), bf16)
    hidden, grad_pre, keep, send = call(
        ends_kernel,
        (rows, rows, SDS((16, 80, 128), f32), SDS((16, 80, 128), bf16)),
        core,
        full,
        up_weight,
        down_weight,
    )
    ends = (keep + lax.ppermute(send, "c", SWAP).astype(f32)).astype(bf16)
    out_block = SDS((count // 16, width), bf16)
    output, input_grad = call(total_kernel, (out_block, out_block), trade(ends, ("dp", "z")))
    both = both.reshape(2, 2, count, width)
    acts, cots = both[:, 0].reshape(2 * count, width), both[:, 1].reshape(2 * count, width)
    up_grad = dot(acts, grad_pre, ((0,), (0,))).astype(bf16)
    down_grad = dot(hidden, cots, ((0,), (0,))).astype(bf16)
    return output, input_grad, up_grad, down_grad


def solution(mesh):
    fine = Mesh(mesh.devices.reshape(2, 2, 8, 8, 2), ("dp", "xh", "y", "z", "c"))
    split = ("dp", "z", "c")
    acts, up, down = P("dp", ROW), P(ROW, split), P(split, ROW)
    return jax.shard_map(
        body,
        mesh=fine,
        in_specs=(acts, acts, up, down),
        out_specs=(down, down, up, down),
        check_vma=False,
    )
```

```python
import jax
import jax.numpy as jnp
from jax import lax
from jax.experimental import pallas as pl
from jax.experimental.pallas import tpu as pltpu
from jax.sharding import Mesh, PartitionSpec as P

Y, PEERS, ROW = ("yh", "yl"), ("xh", "yh"), ("xh", "yh", "yl")
f32, bf16 = jnp.float32, jnp.bfloat16
SDS = jax.ShapeDtypeStruct


def dot(a, b, dims):
    return lax.dot_general(a, b, (dims, ((), ())), preferred_element_type=f32)


def call(kernel, outs, *args):
    spaces = [pltpu.SMEM if a.dtype == jnp.int32 else pltpu.VMEM for a in args]
    return pl.pallas_call(
        kernel,
        out_shape=outs,
        in_specs=[pl.BlockSpec(memory_space=s) for s in spaces],
        compiler_params=pltpu.CompilerParams(vmem_limit_bytes=24 * 2**20),
    )(*args)


def low(shape):
    return lax.broadcasted_iota(jnp.int32, shape, 0) < 4


def spots(d, j):
    return (24 * j, 16 * j) if d == 0 else (96 + 16 * j, 64 + 24 * j)


def place(refs, d, j, hid, grad, tail):
    h, g = spots(d, j)
    refs[0][h : h + 16] = hid.astype(refs[0].dtype)
    refs[1][g : g + 16] = grad.astype(refs[1].dtype)
    at = (h, g)[d] + 16
    refs[d][at : at + 8] = tail.astype(refs[d].dtype)


def take(refs, d, j):
    h, g = spots(d, j)
    at = (h, g)[d] + 16
    hid, grad, tail = refs[0][h : h + 16], refs[1][g : g + 16], refs[d][at : at + 8]
    return hid.astype(f32), grad.astype(f32), tail.astype(f32)


def order_rows(rows):
    n = rows.shape[0]
    i = lax.broadcasted_iota(jnp.int32, (n, n), 0)
    t = lax.broadcasted_iota(jnp.int32, (n, n), 1)
    k = i - n * 4 // 5
    source = jnp.where(k < 0, 10 * (i >> 3) + (i & 7), 10 * (k >> 1) + 8 + (k & 1))
    return dot((source == t).astype(f32).astype(bf16), rows, ((1,), (0,))).astype(bf16)


def partial_kernel(side_ref, both_ref, up_ref, down_ref, acts_ref, cots_ref, keep_h, keep_g, send_h, send_g):
    even = side_ref[0] == 0
    for d in range(2):
        at, rows = 320 * d, slice(160 * d, 160 * d + 160)
        acts_ref[rows] = order_rows(both_ref[at : at + 160])
        cots_ref[rows] = order_rows(both_ref[at + 160 : at + 320])
        up = dot(acts_ref[rows], up_ref[...], ((1,), (0,)))
        back = dot(cots_ref[rows], down_ref[...], ((1,), (1,)))
        for j in range(4):
            m, n = slice(32 * j, 32 * j + 16), slice(32 * j + 16, 32 * j + 32)
            u, b = up[128 + 8 * j : 136 + 8 * j], back[128 + 8 * j : 136 + 8 * j]
            first = low(u.shape)
            near = up[m], back[m], jnp.where(first, u, pltpu.roll(b, 4, 0))
            far = up[n], back[n], jnp.where(first, pltpu.roll(u, 4, 0), b)
            place((keep_h, keep_g), d, j, *(jnp.where(even, x, y) for x, y in zip(near, far)))
            place((send_h, send_g), d, j, *(jnp.where(even, y, x) for x, y in zip(near, far)))


def merge_kernel(keep_h, keep_g, recv_h, recv_g, out_ref):
    for d in range(2):
        for j in range(4):
            own, got = take((keep_h, keep_g), d, j), take((recv_h, recv_g), d, j)
            hid, grad, tail = ((a + b).astype(bf16) for a, b in zip(own, got))
            out_ref[4 * d + j, 0:16] = hid
            out_ref[4 * d + j, 16:32] = grad
            out_ref[4 * d + j, 32:40] = tail


def split_kernel(full_ref, send_h, send_g):
    for d in range(2):
        for j in range(4):
            slab = full_ref.at[4 * d + j]
            place((send_h, send_g), d, j, slab[0:16], slab[16:32], slab[32:40])


def gate(pre, back):
    sigma = 1.0 / (1.0 + jnp.exp(-pre))
    return pre * sigma, back * (sigma * (1.0 + pre * (1.0 - sigma)))


def activate_kernel(parts_ref, out_ref):
    terms = [parts_ref[i].astype(f32) for i in range(8)]
    while len(terms) > 1:
        terms = [a + b for a, b in zip(terms[::2], terms[1::2])]
    sums = terms[0].astype(bf16).astype(f32)
    hidden, grad = gate(sums[0:16], sums[16:32])
    tail = sums[32:40]
    tail_hidden, tail_grad = gate(tail, pltpu.roll(tail, 4, 0))
    tail = jnp.where(low(tail.shape), tail_hidden, pltpu.roll(tail_grad, 4, 0)).astype(bf16)
    hidden, grad = hidden.astype(bf16), grad.astype(bf16)
    for i in range(8):
        out_ref[i, 0:16] = hidden
        out_ref[i, 16:32] = grad
        out_ref[i, 32:40] = tail


def ends_kernel(core_ref, side_ref, full_ref, recv_h, recv_g, up_ref, down_ref, hid_ref, grad_ref, keep_ref, send_ref):
    is_even = side_ref[0] == 0
    for d in range(2):
        base = 160 * d
        hids, grads = [], []
        for j in range(4):
            slab = full_ref.at[4 * d + j]
            own = [slab[0:16].astype(f32), slab[16:32].astype(f32), slab[32:40].astype(f32)]
            got = take((recv_h, recv_g), d, j)
            for k, (one, two) in enumerate(((own, got), (got, own))):
                at = base + 32 * j + 16 * k
                hid_ref[at : at + 16] = jnp.where(is_even, one[0], two[0]).astype(bf16)
                grad_ref[at : at + 16] = jnp.where(is_even, one[1], two[1]).astype(bf16)
            even, odd = jnp.where(is_even, own[2], got[2]), jnp.where(is_even, got[2], own[2])
            first = low(even.shape)
            hids.append(jnp.where(first, even, pltpu.roll(odd, 4, 0)))
            grads.append(jnp.where(first, pltpu.roll(even, 4, 0), odd))
        hid_ref[base + 128 : base + 160] = jnp.concatenate(hids).astype(bf16)
        grad_ref[base + 128 : base + 160] = jnp.concatenate(grads).astype(bf16)
    near = core_ref[0] == 0
    pair = lax.broadcasted_iota(jnp.int32, (8, 128), 0) >> 1
    for d in range(2):
        rows = slice(160 * d, 160 * d + 160)
        out = dot(hid_ref[rows], down_ref[...], ((1,), (0,)))
        inp = dot(grad_ref[rows], up_ref[...], ((1,), (1,)))
        for k in range(8):
            r = 8 * d + k
            at = 128 + 8 * (k // 2)
            for part, full in enumerate((out, inp)):
                tails = [jnp.zeros((8, 128), f32)] * 2
                for l in range(4):
                    lanes = slice(128 * l, 128 * l + 128)
                    to = 32 * part + 8 * l
                    a, b = full[16 * k : 16 * k + 8, lanes], full[16 * k + 8 : 16 * k + 16, lanes]
                    keep_ref[r, to : to + 8] = jnp.where(near, a, b)
                    send_ref[r, to : to + 8] = jnp.where(near, b, a).astype(bf16)
                    tile = full[at : at + 8, lanes]
                    for c in range(2):
                        shift = (2 * l - 2 * c - 4 * (k % 2)) % 8
                        moved = pltpu.roll(tile, shift, 0) if shift else tile
                        tails[c] = jnp.where(pair == l, moved, tails[c])
                to = 64 + 8 * part
                keep_ref[r, to : to + 8] = jnp.where(near, tails[0], tails[1])
                send_ref[r, to : to + 8] = jnp.where(near, tails[1], tails[0]).astype(bf16)


def total_kernel(parts_ref, out_ref, inp_ref):
    terms = [parts_ref[i].astype(f32) for i in range(16)]
    while len(terms) > 1:
        terms = [a + b for a, b in zip(terms[::2], terms[1::2])]
    sums = terms[0]
    for part, ref in enumerate((out_ref, inp_ref)):
        tail = sums[64 + 8 * part : 72 + 8 * part]
        for l in range(4):
            to = 32 * part + 8 * l
            last = pltpu.roll(tail, 8 - 2 * l, 0) if l else tail
            rows = jnp.concatenate([sums[to : to + 8], last]).astype(bf16)
            ref[:, 128 * l : 128 * l + 128] = rows[:10]


def trade(parts, axis):
    return lax.all_to_all(parts, axis, 0, 0, tiled=True)


def core_kernel(core_ref, keep_ref, cores_ref, out_ref):
    out_ref[...] = (keep_ref[...] + cores_ref[1 - core_ref[0]].astype(f32)).astype(bf16)


def neighbours(to_up, to_down):
    up = lax.ppermute(to_up, Y, [(i, (i + 1) % 8) for i in range(8)])
    return up, lax.ppermute(to_down, Y, [(i, (i - 1) % 8) for i in range(8)])


def body(tokens, cotangent, up_weight, down_weight):
    core, side = lax.axis_index("c")[None], lax.axis_index("yl")[None]
    count, width = tokens.shape
    hid = up_weight.shape[1]
    both = lax.all_gather(jnp.concatenate([tokens, cotangent]), "dp", axis=0, tiled=True)
    both, core, side = lax.optimization_barrier((both, core, side))
    wide, note = SDS((160, hid), f32), SDS((160, hid), bf16)
    ordered = SDS((2 * count, width), bf16)
    outs = (ordered, ordered, wide, wide, note, note)
    acts, cots, *keep, to_up, to_down = call(partial_kernel, outs, side, both, up_weight, down_weight)
    slabs = SDS((8, 40, hid), bf16)
    parts = trade(call(merge_kernel, slabs, *keep, *neighbours(to_up, to_down)), PEERS)
    full = trade(call(activate_kernel, slabs, parts), PEERS)
    others = neighbours(*call(split_kernel, (note, note), full))
    rows = SDS((2 * count, hid), bf16)
    hidden, grad_pre, keep, send = call(
        ends_kernel,
        (rows, rows, SDS((16, 80, 128), f32), SDS((16, 80, 128), bf16)),
        core,
        side,
        full,
        *others,
        up_weight,
        down_weight,
    )
    cores = lax.all_gather(send, "c", axis=0)
    ends = trade(call(core_kernel, SDS(send.shape, bf16), core, keep, cores), ("dp", "z"))
    out_block = SDS((count // 16, width), bf16)
    output, input_grad = call(total_kernel, (out_block, out_block), ends)
    up_grad = dot(acts, grad_pre, ((0,), (0,))).astype(bf16)
    down_grad = dot(hidden, cots, ((0,), (0,))).astype(bf16)
    return output, input_grad, up_grad, down_grad


def solution(mesh):
    fine = Mesh(mesh.devices.reshape(2, 2, 4, 2, 8, 2), ("dp", "xh", "yh", "yl", "z", "c"))
    split = ("dp", "z", "c")
    acts, up, down = P("dp", ROW), P(ROW, split), P(split, ROW)
    return jax.shard_map(
        body,
        mesh=fine,
        in_specs=(acts, acts, up, down),
        out_specs=(down, down, up, down),
        check_vma=False,
    )
```

```python
import jax
import jax.numpy as jnp
from jax import lax
from jax.experimental import pallas as pl
from jax.experimental.pallas import tpu as pltpu
from jax.sharding import Mesh, PartitionSpec as P

Y, PEERS, ROW = ("yh", "yl"), ("xh", "yh"), ("xh", "yh", "yl")
f32, bf16 = jnp.float32, jnp.bfloat16
SDS = jax.ShapeDtypeStruct


def dot(a, b, dims):
    return lax.dot_general(a, b, (dims, ((), ())), preferred_element_type=f32)


def call(kernel, outs, *args):
    return pl.pallas_call(
        kernel,
        out_shape=outs,
        in_specs=[pl.BlockSpec(memory_space=pltpu.SMEM) if a.dtype == jnp.int32 else pl.BlockSpec() for a in args],
        compiler_params=pltpu.CompilerParams(vmem_limit_bytes=24 * 2**20),
    )(*args)


def low(shape):
    return lax.broadcasted_iota(jnp.int32, shape, 0) < 4


def spots(d, j):
    return (24 * j, 16 * j) if d == 0 else (16 * j, 24 * j)


def halves(refs, d):
    return (refs[0].at[0:96], refs[1].at[0:64]) if d == 0 else (refs[0].at[96:160], refs[1].at[64:160])


def place(refs, d, j, hid, grad, tail):
    h, g = spots(d, j)
    refs[0][h : h + 16] = hid.astype(refs[0].dtype)
    refs[1][g : g + 16] = grad.astype(refs[1].dtype)
    at = (h, g)[d] + 16
    refs[d][at : at + 8] = tail.astype(refs[d].dtype)


def take(refs, d, j):
    h, g = spots(d, j)
    at = (h, g)[d] + 16
    hid, grad, tail = refs[0][h : h + 16], refs[1][g : g + 16], refs[d][at : at + 8]
    return hid.astype(f32), grad.astype(f32), tail.astype(f32)


def group(dp_ref, i):
    return dp_ref[0] if i == 0 else 1 - dp_ref[0]


def order_rows(rows):
    n = rows.shape[0]
    i = lax.broadcasted_iota(jnp.int32, (n, n), 0)
    t = lax.broadcasted_iota(jnp.int32, (n, n), 1)
    k = i - n * 4 // 5
    source = jnp.where(k < 0, 10 * (i >> 3) + (i & 7), 10 * (k >> 1) + 8 + (k & 1))
    return dot((source == t).astype(f32).astype(bf16), rows, ((1,), (0,))).astype(bf16)


def partial_kernel(side_ref, both_ref, up_ref, down_ref, acts_ref, cots_ref, keep_ref, send_ref):
    even = side_ref[0] == 0
    acts_ref[...] = order_rows(both_ref[0:160])
    cots_ref[...] = order_rows(both_ref[160:320])
    up = dot(acts_ref[...], up_ref[...], ((1,), (0,)))
    back = dot(cots_ref[...], down_ref[...], ((1,), (1,)))
    for j in range(4):
        m, n = slice(32 * j, 32 * j + 16), slice(32 * j + 16, 32 * j + 32)
        u, b = up[128 + 8 * j : 136 + 8 * j], back[128 + 8 * j : 136 + 8 * j]
        first = low(u.shape)
        near = up[m], back[m], jnp.where(first, u, pltpu.roll(b, 4, 0))
        far = up[n], back[n], jnp.where(first, pltpu.roll(u, 4, 0), b)
        for x, y, at, size in zip(near, far, (0, 16, 32), (16, 16, 8)):
            at = slice(40 * j + at, 40 * j + at + size)
            keep_ref[at] = jnp.where(even, x, y)
            send_ref[at] = jnp.where(even, y, x).astype(bf16)


def merge_kernel(dp_ref, keep_own, keep_far, recv_own, recv_far, out_ref):
    for i, (keep, recv) in enumerate(((keep_own, recv_own), (keep_far, recv_far))):
        for j in range(4):
            at = slice(40 * j, 40 * j + 40)
            out_ref[4 * group(dp_ref, i) + j] = (keep[at] + recv[at].astype(f32)).astype(bf16)


def split_kernel(full_ref, send_h, send_g):
    for d in range(2):
        for j in range(4):
            slab = full_ref.at[4 * d + j]
            place(halves((send_h, send_g), d), d, j, slab[0:16], slab[16:32], slab[32:40])


def gate(pre, back):
    sigma = 1.0 / (1.0 + jnp.exp(-pre))
    return pre * sigma, back * (sigma * (1.0 + pre * (1.0 - sigma)))


def activate_kernel(parts_ref, out_ref):
    terms = [parts_ref[i].astype(f32) for i in range(8)]
    while len(terms) > 1:
        terms = [a + b for a, b in zip(terms[::2], terms[1::2])]
    sums = terms[0].astype(bf16).astype(f32)
    hidden, grad = gate(sums[0:16], sums[16:32])
    tail = sums[32:40]
    tail_hidden, tail_grad = gate(tail, pltpu.roll(tail, 4, 0))
    tail = jnp.where(low(tail.shape), tail_hidden, pltpu.roll(tail_grad, 4, 0)).astype(bf16)
    hidden, grad = hidden.astype(bf16), grad.astype(bf16)
    for i in range(8):
        out_ref[i, 0:16] = hidden
        out_ref[i, 16:32] = grad
        out_ref[i, 32:40] = tail


def ends_kernel(core_ref, side_ref, dp_ref, full_ref, recv_h, recv_g, up_ref, down_ref, hid_ref, grad_ref, keep_ref, send_ref):
    is_even = side_ref[0] == 0
    for d in range(2):
        base = pl.multiple_of(160 * group(dp_ref, d), 32)
        hids, grads = [], []
        for j in range(4):
            slab = full_ref.at[4 * d + j]
            own = [slab[0:16].astype(f32), slab[16:32].astype(f32), slab[32:40].astype(f32)]
            got = take(halves((recv_h, recv_g), d), d, j)
            for k, (one, two) in enumerate(((own, got), (got, own))):
                at = pl.ds(base + (32 * j + 16 * k), 16)
                hid_ref[at] = jnp.where(is_even, one[0], two[0]).astype(bf16)
                grad_ref[at] = jnp.where(is_even, one[1], two[1]).astype(bf16)
            even, odd = jnp.where(is_even, own[2], got[2]), jnp.where(is_even, got[2], own[2])
            first = low(even.shape)
            hids.append(jnp.where(first, even, pltpu.roll(odd, 4, 0)))
            grads.append(jnp.where(first, pltpu.roll(even, 4, 0), odd))
        hid_ref[pl.ds(base + 128, 32)] = jnp.concatenate(hids).astype(bf16)
        grad_ref[pl.ds(base + 128, 32)] = jnp.concatenate(grads).astype(bf16)
    near = core_ref[0] == 0
    pair = lax.broadcasted_iota(jnp.int32, (8, 128), 0) >> 1
    for d in range(2):
        rows = pl.ds(pl.multiple_of(160 * group(dp_ref, d), 32), 160)
        out = dot(hid_ref[rows], down_ref[...], ((1,), (0,)))
        inp = dot(grad_ref[rows], up_ref[...], ((1,), (1,)))
        for k in range(8):
            r = 8 * d + k
            at = 128 + 8 * (k // 2)
            for part, full in enumerate((out, inp)):
                tails = [jnp.zeros((8, 128), f32)] * 2
                for l in range(4):
                    lanes = slice(128 * l, 128 * l + 128)
                    to = 32 * part + 8 * l
                    a, b = full[16 * k : 16 * k + 8, lanes], full[16 * k + 8 : 16 * k + 16, lanes]
                    keep_ref[r, to : to + 8] = jnp.where(near, a, b)
                    send_ref[r, to : to + 8] = jnp.where(near, b, a).astype(bf16)
                    tile = full[at : at + 8, lanes]
                    for c in range(2):
                        shift = (2 * l - 2 * c - 4 * (k % 2)) % 8
                        moved = pltpu.roll(tile, shift, 0) if shift else tile
                        tails[c] = jnp.where(pair == l, moved, tails[c])
                to = 64 + 8 * part
                keep_ref[r, to : to + 8] = jnp.where(near, tails[0], tails[1])
                send_ref[r, to : to + 8] = jnp.where(near, tails[1], tails[0]).astype(bf16)


def total_kernel(parts_ref, out_ref, inp_ref):
    terms = [parts_ref[i].astype(f32) for i in range(16)]
    while len(terms) > 1:
        terms = [a + b for a, b in zip(terms[::2], terms[1::2])]
    sums = terms[0]
    for part, ref in enumerate((out_ref, inp_ref)):
        tail = sums[64 + 8 * part : 72 + 8 * part]
        for l in range(4):
            to = 32 * part + 8 * l
            last = pltpu.roll(tail, 8 - 2 * l, 0) if l else tail
            rows = jnp.concatenate([sums[to : to + 8], last]).astype(bf16)
            ref[:, 128 * l : 128 * l + 128] = rows[:10]


def trade(parts, axis):
    return lax.all_to_all(parts, axis, 0, 0, tiled=True)


def core_kernel(core_ref, keep_ref, cores_ref, out_ref):
    out_ref[...] = (keep_ref[...] + cores_ref[1 - core_ref[0]].astype(f32)).astype(bf16)


def neighbour(rows, step):
    return lax.ppermute(rows, Y, [(i, (i + step) % 8) for i in range(8)])


def body(tokens, cotangent, up_weight, down_weight):
    core, side, dp = (lax.axis_index(n)[None] for n in ("c", "yl", "dp"))
    count, width = tokens.shape
    hid = up_weight.shape[1]
    both = jnp.concatenate([tokens, cotangent])
    both, core, side, dp = lax.optimization_barrier((both, core, side, dp))
    far = lax.ppermute(both, "dp", [(0, 1), (1, 0)])
    ordered = SDS((count, width), bf16)
    acts, cots, keep, recv = [], [], [], []
    for i, rows in enumerate((both, far)):
        outs = ordered, ordered, SDS((160, hid), f32), SDS((160, hid), bf16)
        ours, theirs, mine, sent = call(partial_kernel, outs, side, rows, up_weight, down_weight)
        acts.append(ours)
        cots.append(theirs)
        keep.append(mine)
        recv.append(neighbour(sent, 1 - 2 * i))
    acts, cots = jnp.concatenate(acts), jnp.concatenate(cots)
    note = SDS((160, hid), bf16)
    slabs = SDS((8, 40, hid), bf16)
    parts = trade(call(merge_kernel, slabs, dp, *keep, *recv), PEERS)
    full = trade(call(activate_kernel, slabs, parts), PEERS)
    to_up, to_down = call(split_kernel, (note, note), full)
    others = neighbour(to_up, 1), neighbour(to_down, -1)
    rows = SDS((2 * count, hid), bf16)
    hidden, grad_pre, keep, send = call(
        ends_kernel,
        (rows, rows, SDS((16, 80, 128), f32), SDS((16, 80, 128), bf16)),
        core,
        side,
        dp,
        full,
        *others,
        up_weight,
        down_weight,
    )
    cores = lax.all_gather(send, "c", axis=0)
    ends = trade(call(core_kernel, SDS(send.shape, bf16), core, keep, cores), ("dp", "z"))
    out_block = SDS((count // 16, width), bf16)
    output, input_grad = call(total_kernel, (out_block, out_block), ends)
    up_grad = dot(acts, grad_pre, ((0,), (0,))).astype(bf16)
    down_grad = dot(hidden, cots, ((0,), (0,))).astype(bf16)
    return output, input_grad, up_grad, down_grad


def solution(mesh):
    fine = Mesh(mesh.devices.reshape(2, 2, 4, 2, 8, 2), ("dp", "xh", "yh", "yl", "z", "c"))
    split = ("dp", "z", "c")
    acts, up, down = P("dp", ROW), P(ROW, split), P(split, ROW)
    return jax.shard_map(
        body,
        mesh=fine,
        in_specs=(acts, acts, up, down),
        out_specs=(down, down, up, down),
        check_vma=False,
    )
```

```python
import jax
import jax.numpy as jnp
from jax import lax
from jax.experimental import pallas as pl
from jax.experimental.pallas import tpu as pltpu
from jax.sharding import Mesh, PartitionSpec as P

Y, PEERS, ROW = ("yh", "yl"), ("yh", "xh"), ("xh", "yh", "yl")
f32, bf16 = jnp.float32, jnp.bfloat16
SDS = jax.ShapeDtypeStruct


def dot(a, b, dims):
    return lax.dot_general(a, b, (dims, ((), ())), preferred_element_type=f32)


def call(kernel, outs, *args):
    return pl.pallas_call(
        kernel,
        out_shape=outs,
        in_specs=[pl.BlockSpec(memory_space=pltpu.SMEM) if a.dtype == jnp.int32 else pl.BlockSpec() for a in args],
        compiler_params=pltpu.CompilerParams(vmem_limit_bytes=24 * 2**20),
    )(*args)


def low(shape):
    return lax.broadcasted_iota(jnp.int32, shape, 0) < 4


def spots(d, j):
    return (24 * j, 16 * j) if d == 0 else (16 * j, 24 * j)


def halves(refs, d):
    return (refs[0].at[0:96], refs[1].at[0:64]) if d == 0 else (refs[0].at[96:160], refs[1].at[64:160])


def place(refs, d, j, hid, grad, tail):
    h, g = spots(d, j)
    refs[0][h : h + 16] = hid.astype(refs[0].dtype)
    refs[1][g : g + 16] = grad.astype(refs[1].dtype)
    at = (h, g)[d] + 16
    refs[d][at : at + 8] = tail.astype(refs[d].dtype)


def take(refs, d, j):
    h, g = spots(d, j)
    at = (h, g)[d] + 16
    hid, grad, tail = refs[0][h : h + 16], refs[1][g : g + 16], refs[d][at : at + 8]
    return hid.astype(f32), grad.astype(f32), tail.astype(f32)


def group(dp_ref, i):
    return dp_ref[0] if i == 0 else 1 - dp_ref[0]


def order_rows(rows):
    n = rows.shape[0]
    i = lax.broadcasted_iota(jnp.int32, (n, n), 0)
    t = lax.broadcasted_iota(jnp.int32, (n, n), 1)
    k = i - n * 4 // 5
    source = jnp.where(k < 0, 10 * (i >> 3) + (i & 7), 10 * (k >> 1) + 8 + (k & 1))
    return dot((source == t).astype(f32).astype(bf16), rows, ((1,), (0,))).astype(bf16)


def partial_kernel(side_ref, both_ref, up_ref, down_ref, acts_ref, cots_ref, keep_ref, send_ref):
    even = side_ref[0] == 0
    acts_ref[...] = order_rows(both_ref[0:160])
    cots_ref[...] = order_rows(both_ref[160:320])
    up = dot(acts_ref[...], up_ref[...], ((1,), (0,)))
    back = dot(cots_ref[...], down_ref[...], ((1,), (1,)))
    for j in range(4):
        m, n = slice(32 * j, 32 * j + 16), slice(32 * j + 16, 32 * j + 32)
        u, b = up[128 + 8 * j : 136 + 8 * j], back[128 + 8 * j : 136 + 8 * j]
        first = low(u.shape)
        near = up[m], back[m], jnp.where(first, u, pltpu.roll(b, 4, 0))
        far = up[n], back[n], jnp.where(first, pltpu.roll(u, 4, 0), b)
        for x, y, at, size in zip(near, far, (0, 16, 32), (16, 16, 8)):
            at = slice(40 * j + at, 40 * j + at + size)
            keep_ref[at] = jnp.where(even, x, y)
            send_ref[at] = jnp.where(even, y, x).astype(bf16)


def merge_kernel(dp_ref, keep_own, keep_far, recv_own, recv_far, out_ref):
    for i, (keep, recv) in enumerate(((keep_own, recv_own), (keep_far, recv_far))):
        for j in range(4):
            at = slice(40 * j, 40 * j + 40)
            out_ref[2 * j + group(dp_ref, i)] = (keep[at] + recv[at].astype(f32)).astype(bf16)


def split_kernel(full_ref, send_h, send_g):
    for d in range(2):
        for j in range(4):
            slab = full_ref.at[2 * j + d]
            place(halves((send_h, send_g), d), d, j, slab[0:16], slab[16:32], slab[32:40])


def gate(pre, back):
    sigma = 1.0 / (1.0 + jnp.exp(-pre))
    return pre * sigma, back * (sigma * (1.0 + pre * (1.0 - sigma)))


def activate_kernel(parts_ref, out_ref):
    terms = [parts_ref[i].astype(f32) for i in range(8)]
    while len(terms) > 1:
        terms = [a + b for a, b in zip(terms[::2], terms[1::2])]
    sums = terms[0].astype(bf16).astype(f32)
    hidden, grad = gate(sums[0:16], sums[16:32])
    tail = sums[32:40]
    tail_hidden, tail_grad = gate(tail, pltpu.roll(tail, 4, 0))
    tail = jnp.where(low(tail.shape), tail_hidden, pltpu.roll(tail_grad, 4, 0)).astype(bf16)
    hidden, grad = hidden.astype(bf16), grad.astype(bf16)
    for i in range(8):
        out_ref[i, 0:16] = hidden
        out_ref[i, 16:32] = grad
        out_ref[i, 32:40] = tail


def ends_kernel(core_ref, side_ref, dp_ref, full_ref, recv_h, recv_g, up_ref, down_ref, hid_ref, grad_ref, keep_ref, send_ref):
    is_even = side_ref[0] == 0
    for d in range(2):
        base = pl.multiple_of(160 * group(dp_ref, d), 32)
        hids, grads = [], []
        for j in range(4):
            slab = full_ref.at[2 * j + d]
            own = [slab[0:16].astype(f32), slab[16:32].astype(f32), slab[32:40].astype(f32)]
            got = take(halves((recv_h, recv_g), d), d, j)
            for k, (one, two) in enumerate(((own, got), (got, own))):
                at = pl.ds(base + (32 * j + 16 * k), 16)
                hid_ref[at] = jnp.where(is_even, one[0], two[0]).astype(bf16)
                grad_ref[at] = jnp.where(is_even, one[1], two[1]).astype(bf16)
            even, odd = jnp.where(is_even, own[2], got[2]), jnp.where(is_even, got[2], own[2])
            first = low(even.shape)
            hids.append(jnp.where(first, even, pltpu.roll(odd, 4, 0)))
            grads.append(jnp.where(first, pltpu.roll(even, 4, 0), odd))
        hid_ref[pl.ds(base + 128, 32)] = jnp.concatenate(hids).astype(bf16)
        grad_ref[pl.ds(base + 128, 32)] = jnp.concatenate(grads).astype(bf16)
    near = core_ref[0] == 0
    pair = lax.broadcasted_iota(jnp.int32, (8, 128), 0) >> 1
    for d in range(2):
        rows = pl.ds(pl.multiple_of(160 * group(dp_ref, d), 32), 160)
        out = dot(hid_ref[rows], down_ref[...], ((1,), (0,)))
        inp = dot(grad_ref[rows], up_ref[...], ((1,), (1,)))
        for k in range(8):
            r = 8 * d + k
            at = 128 + 8 * (k // 2)
            for part, full in enumerate((out, inp)):
                tails = [jnp.zeros((8, 128), f32)] * 2
                for l in range(4):
                    lanes = slice(128 * l, 128 * l + 128)
                    to = 32 * part + 8 * l
                    a, b = full[16 * k : 16 * k + 8, lanes], full[16 * k + 8 : 16 * k + 16, lanes]
                    keep_ref[r, to : to + 8] = jnp.where(near, a, b)
                    send_ref[r, to : to + 8] = jnp.where(near, b, a).astype(bf16)
                    tile = full[at : at + 8, lanes]
                    for c in range(2):
                        shift = (2 * l - 2 * c - 4 * (k % 2)) % 8
                        moved = pltpu.roll(tile, shift, 0) if shift else tile
                        tails[c] = jnp.where(pair == l, moved, tails[c])
                to = 64 + 8 * part
                keep_ref[r, to : to + 8] = jnp.where(near, tails[0], tails[1])
                send_ref[r, to : to + 8] = jnp.where(near, tails[1], tails[0]).astype(bf16)


def total_kernel(parts_ref, out_ref, inp_ref):
    terms = [parts_ref[i].astype(f32) for i in range(16)]
    while len(terms) > 1:
        terms = [a + b for a, b in zip(terms[::2], terms[1::2])]
    sums = terms[0]
    for part, ref in enumerate((out_ref, inp_ref)):
        tail = sums[64 + 8 * part : 72 + 8 * part]
        for l in range(4):
            to = 32 * part + 8 * l
            last = pltpu.roll(tail, 8 - 2 * l, 0) if l else tail
            rows = jnp.concatenate([sums[to : to + 8], last]).astype(bf16)
            ref[:, 128 * l : 128 * l + 128] = rows[:10]


def trade(parts, axis):
    return lax.all_to_all(parts, axis, 0, 0, tiled=True)


def core_kernel(core_ref, keep_ref, cores_ref, out_ref):
    out_ref[...] = (keep_ref[...] + cores_ref[1 - core_ref[0]].astype(f32)).astype(bf16)


def neighbour(rows, step):
    return lax.ppermute(rows, Y, [(i, (i + step) % 8) for i in range(8)])


def across(rows, first):
    ways = [(y, c, (y + (1 if c == first else -1)) % 8) for y in range(8) for c in range(2)]
    return lax.ppermute(rows, ("yh", "yl", "c"), [(2 * y + c, 2 * to + c) for y, c, to in ways])


def body(tokens, cotangent, up_weight, down_weight):
    core, side, dp = (lax.axis_index(n)[None] for n in ("c", "yl", "dp"))
    count, width = tokens.shape
    hid = up_weight.shape[1]
    both = jnp.concatenate([tokens, cotangent])
    both, core, side, dp = lax.optimization_barrier((both, core, side, dp))
    far = lax.ppermute(both, "dp", [(0, 1), (1, 0)])
    ordered = SDS((count, width), bf16)
    acts, cots, keep, recv = [], [], [], []
    for i, rows in enumerate((both, far)):
        outs = ordered, ordered, SDS((160, hid), f32), SDS((160, hid), bf16)
        ours, theirs, mine, sent = call(partial_kernel, outs, side, rows, up_weight, down_weight)
        acts.append(ours)
        cots.append(theirs)
        keep.append(mine)
        recv.append(across(sent, i))
    acts, cots = jnp.concatenate(acts), jnp.concatenate(cots)
    note = SDS((160, hid), bf16)
    slabs = SDS((8, 40, hid), bf16)
    parts = trade(call(merge_kernel, slabs, dp, *keep, *recv), PEERS)
    full = trade(call(activate_kernel, slabs, parts), PEERS)
    to_up, to_down = call(split_kernel, (note, note), full)
    others = neighbour(to_up, 1), neighbour(to_down, -1)
    rows = SDS((2 * count, hid), bf16)
    hidden, grad_pre, keep, send = call(
        ends_kernel,
        (rows, rows, SDS((16, 80, 128), f32), SDS((16, 80, 128), bf16)),
        core,
        side,
        dp,
        full,
        *others,
        up_weight,
        down_weight,
    )
    cores = lax.all_gather(send, "c", axis=0)
    ends = trade(call(core_kernel, SDS(send.shape, bf16), core, keep, cores), ("dp", "z"))
    out_block = SDS((count // 16, width), bf16)
    output, input_grad = call(total_kernel, (out_block, out_block), ends)
    up_grad = dot(acts, grad_pre, ((0,), (0,))).astype(bf16)
    down_grad = dot(hidden, cots, ((0,), (0,))).astype(bf16)
    return output, input_grad, up_grad, down_grad


def solution(mesh):
    fine = Mesh(mesh.devices.reshape(2, 2, 4, 2, 8, 2), ("dp", "xh", "yh", "yl", "z", "c"))
    split = ("dp", "z", "c")
    acts, up, down = P("dp", ROW), P(ROW, split), P(split, ROW)
    return jax.shard_map(
        body,
        mesh=fine,
        in_specs=(acts, acts, up, down),
        out_specs=(down, down, up, down),
        check_vma=False,
    )
```
